32 devices in a mesh: row: 4 (over x, core), col: 2 (over y), layer: 4 (over z).
Axes of the slice: x: 2, y: 2, z: 4, core: 2. Of those that a mesh axis runs over, the one named last changes fastest.
Arguments:
- density_matrix: bfloat16 [2048, 2048], P('row', 'col'), may hold values from -3 to 3
- block_mask: int32 [32, 32], P('row', 'col'), may hold values 0 or 1
- intersection_weights: float32 [2048], P(('col', 'layer')), may hold values from -0.125 to 0.125
- exponents: float32 [2048], P('row'), may hold values from 0.5 to 8
- anchor_x: int32 [32], P('row'), may hold values from 0 to 31
- anchor_y: int32 [32], P('row'), may hold values from 0 to 127, as said below
- anchor_z: int32 [32], P('row'), may hold values from 0 to 127
Outputs:
- squared: bfloat16 [2048, 2048], P('row', ('col', 'layer'))
- density: float32 [128, 128, 128], P('row', ('col', 'layer'))
The draws below stay inside these ranges and needn't reach their ends.
Inputs may be any that keep to these rules, and one draw needn't show every extreme that they name: `anchor_y`: block row a starts in the second dimension between (a mod (8)) * 16 and that plus 16 - 1.
All inputs are finite; a program needn't handle non-finite values. No bound on the sum of `block_mask` on one device may be relied on, other than what follows from the above.
Results may differ from the reference program's by a relative error of at most 0.0055.
Values may be sent and summed in bfloat16 or wider, within the bound.
A program may use at most 64 MiB of HBM per device.

```python
import math
import jax
import jax.numpy as jnp
from jax import lax

BLOCK = 64
TILE = 16
APR = 8
SX = 32
SY = 16
GZ = 128
NATOMS = 32
M = 2048
GX = 128
GY = 128


def draw_anchor_y(key, part):
    slab_count = GY // SY
    atom_ids = jnp.arange(NATOMS, dtype=jnp.int32)
    within = jax.random.randint(jax.random.fold_in(key, 11), (NATOMS,), 0, SY, dtype=jnp.int32)
    within = jnp.where(atom_ids == 0, 0, within)
    within = jnp.where(atom_ids == NATOMS - 1, SY - 1, within)
    return (atom_ids % slab_count * SY + within).astype(jnp.int32)


def set_ends(values, rng, smallest, largest):
    longest = values.shape.index(max(values.shape))
    spots = []
    for shift in (0, 1):
        where = [jax.random.randint(jax.random.fold_in(rng, axis), (), 0, length) for axis, length in enumerate(values.shape)]
        where[longest] = (where[longest] + shift) % values.shape[longest]
        spots.append(tuple(where))
    return values.at[spots[0]].set(smallest).at[spots[1]].set(largest)


def steps_of(key, extent, split, smallest, top_value):
    def one(dim, parts):
        draws = jax.random.uniform(jax.random.fold_in(jax.random.fold_in(key, 6), dim), (parts,), jnp.float32, smallest / len(split), top_value / len(split))
        return jnp.repeat(jnp.exp(draws), extent[dim] // parts).reshape((-1,) + (1,) * (len(extent) - dim - 1))

    factor_of = one(*split[0])
    for cut in split[1:]:
        factor_of = factor_of * one(*cut)
    return factor_of


def bell_draw(rng, dims, width, bound, pieces=(), kind=jnp.bfloat16):
    values = jax.random.normal(rng, dims, jnp.float32) * width
    if len(pieces) > 0:
        values = steps_of(rng, dims, pieces, -0.22, 0.18) * values
    return jnp.clip(values, min=-bound, max=bound).astype(kind)


def setup_inputs(seed: int = 0) -> dict:
    keys = jax.random.split(jax.random.key(seed), 8)
    return {
        "density_matrix": bell_draw(keys[0], (M, M), (1.414 / M ** 0.25), 3.0, ((0, 4), (1, 2))),
        "block_mask": set_ends((jax.random.randint(keys[1], (NATOMS, NATOMS), 0, 2) < 1).astype(jnp.int32), jax.random.fold_in(keys[1], 1), 0, 1),
        "intersection_weights": bell_draw(keys[2], (M,), M ** -0.5, 0.125, ((0, 8),), jnp.float32),
        "exponents": jnp.clip(jnp.exp(math.log(8.0) - 2.7725887 * jax.random.uniform(keys[3], (M,), jnp.float32) ** steps_of(keys[3], (M,), ((0, 4),), -0.2, 0.2)), 0.5, 8.0),
        "anchor_x": set_ends(jax.random.randint(keys[4], (NATOMS,), 0, SX), jax.random.fold_in(keys[4], 1), 0, SX - 1).astype(jnp.int32),
        "anchor_y": draw_anchor_y(jax.random.fold_in(keys[7], 71), 0),
        "anchor_z": set_ends(jax.random.randint(keys[6], (NATOMS,), 0, GZ), jax.random.fold_in(keys[6], 1), 0, GZ - 1).astype(jnp.int32),
    }


grid_step_sq = 0.0625


def reference(density_matrix, block_mask, intersection_weights, exponents, anchor_x, anchor_y, anchor_z):
    wide_mask = jnp.repeat(jnp.repeat(block_mask, BLOCK, 0), BLOCK, 1)
    masked = jnp.where(wide_mask > 0, density_matrix, jnp.zeros_like(density_matrix))
    product = jnp.dot(masked, masked, preferred_element_type=jnp.float32)
    squared = product.astype(jnp.bfloat16)
    charges = jnp.dot(product, intersection_weights, precision=lax.Precision.HIGHEST)
    offsets = jnp.arange(TILE, dtype=jnp.int32)
    centre = offsets.astype(jnp.float32) - 7.5

    def deposit(atom_at, grid_now):
        atom_charges = lax.dynamic_slice_in_dim(charges, atom_at * BLOCK, BLOCK)
        decay_rates = lax.dynamic_slice_in_dim(exponents, atom_at * BLOCK, BLOCK)
        profile = jnp.exp(-decay_rates[:, None] * grid_step_sq * centre[None, :] ** 2)
        tile_values = jnp.einsum("k,kx,ky,kz->xyz", atom_charges, profile, profile, profile, precision=lax.Precision.HIGHEST)
        x_cells = ((atom_at // APR) * SX + anchor_x[atom_at] + offsets) % GX
        y_cells = (anchor_y[atom_at] + offsets) % GY
        z_cells = (anchor_z[atom_at] + offsets) % GZ
        return grid_now.at[x_cells[:, None, None], y_cells[None, :, None], z_cells[None, None, :]].add(tile_values)

    density = lax.fori_loop(0, NATOMS, deposit, jnp.zeros((GX, GY, GZ), jnp.float32))
    return squared, density
```

```python
import functools

import jax
import jax.numpy as jnp
from jax import lax
from jax.experimental import pallas as pl
from jax.experimental.pallas import tpu as pltpu
from jax.sharding import PartitionSpec as P

BLOCK = 64
TILE = 16
SX = 32
SY = 16
GZ = 128
STEP_SQ = 0.0625
MESH = pl.DeviceIdType.MESH
F32 = jnp.float32
BF16 = jnp.bfloat16
IN_CHUNKS = 2
OUT_CHUNKS = 4


def dot_nt(a, b):
    return lax.dot_general(a, b, (((1,), (1,)), ((), ())), preferred_element_type=F32)


def hi_lo(x):
    high = x.astype(BF16).astype(F32)
    return jnp.concatenate([high, x - high], axis=0).astype(BF16)


def kernel(
    sizes,
    a_ref, mask_ref, w_ref, e_ref, ax_ref, ay_ref, az_ref,
    sq_ref, den_ref,
    m_buf, right, part_out, part_in, w_all, v_out, v_all, q_out, q_all, pack, pack_in, shape_xy, shape_z,
    piece_send, piece_recv, fwd_send, part_send, part_recv,
    w_send, w_recv, v_send, v_recv, q_send, q_recv, pack_send, pack_recv,
):
    nr, nc, nl = sizes
    ratio = nr // nc
    rows, cols = a_ref.shape
    width = cols // nl
    atoms = rows // BLOCK
    r, c, l = lax.axis_index("row"), lax.axis_index("col"), lax.axis_index("layer")
    sibling = r + 1 - 2 * (r % 2)
    following = (r + 1) % nr

    def remote(src, dst, send, recv, device):
        return pltpu.make_async_remote_copy(
            src_ref=src, dst_ref=dst, send_sem=send, recv_sem=recv,
            device_id=device, device_id_type=MESH,
        )

    barrier = pltpu.get_barrier_semaphore()
    peers = 0
    for dr in range(nr):
        for dc in range(nc):
            if dr or dc:
                peers += 1
                pl.semaphore_signal(
                    barrier, inc=1, device_id=((r + dr) % nr, (c + dc) % nc, l), device_id_type=MESH
                )
    for k in range(1, nl):
        peers += 1
        pl.semaphore_signal(barrier, inc=1, device_id=(r, c, (l + k) % nl), device_id_type=MESH)

    kept = jnp.where(mask_ref[...] > 0, 1.0, 0.0).astype(F32)
    spread = lax.broadcasted_iota(jnp.int32, (cols // BLOCK, cols), 1) // BLOCK
    pick = lax.broadcasted_iota(jnp.int32, (cols // BLOCK, cols), 0)
    wide = jnp.dot(kept, jnp.where(spread == pick, 1.0, 0.0).astype(F32), preferred_element_type=F32)
    for b in range(atoms):
        at = pl.ds(b * BLOCK, BLOCK)
        m_buf[at, :] = a_ref[at, :] * jnp.broadcast_to(wide[b : b + 1, :], (BLOCK, cols)).astype(BF16)
    w_all[l] = jnp.broadcast_to(w_ref[...], (8, width))
    lane_atom = lax.broadcasted_iota(jnp.int32, (8, rows), 1) // BLOCK
    sub = lax.broadcasted_iota(jnp.int32, (8, rows), 0)
    table = jnp.broadcast_to(e_ref[...], (8, rows))
    for j in range(atoms):
        here = lane_atom == j
        for at, ref in ((1, ax_ref), (2, ay_ref), (3, az_ref)):
            table = jnp.where(here & (sub == at), ref[j].astype(F32), table)
    pack[...] = table

    pl.semaphore_wait(barrier, peers)

    w_copies = [
        remote(w_all.at[l], w_all.at[l], w_send.at[k - 1], w_recv.at[k - 1], (r, c, (l + k) % nl))
        for k in range(1, nl)
    ]
    for copy in w_copies:
        copy.start()
    pack_copy = remote(pack, pack_in, pack_send.at[0], pack_recv.at[0], (following, c, l))
    pack_copy.start()

    home = r // ratio
    slot = r % ratio
    step = rows // IN_CHUNKS

    def strip(h):
        return m_buf.at[pl.ds(h * step, step), pl.ds(pl.multiple_of(l * width, 128), width)]

    def piece(i, cc, h):
        return right.at[i, cc, pl.ds(h * step, step), :]

    def sem_at(i, cc, h):
        return (i * nc + cc) * IN_CHUNKS + h

    def piece_copy(k, h):
        return remote(
            strip(h), piece(slot, c, h), piece_send.at[k * IN_CHUNKS + h],
            piece_recv.at[sem_at(slot, c, h)], ((r + 2 * k) % nr, home, l),
        )

    def own_copy(h):
        return pltpu.make_async_copy(strip(h), piece(slot, c, h), piece_recv.at[sem_at(slot, c, h)])

    at_home = home == c
    for h in range(IN_CHUNKS):
        for k in range(1, nr // 2):
            piece_copy(k, h).start()

        @pl.when(at_home)
        def _():
            own_copy(h).start()

        @pl.when(jnp.logical_not(at_home))
        def _():
            piece_copy(0, h).start()

    for copy in w_copies:
        copy.wait_recv()
    total = jnp.zeros((16, rows), F32)
    for k in range(nl):
        total = total + dot_nt(hi_lo(w_all[k]), m_buf[:, k * width : (k + 1) * width])
    v_out[...] = total[:8] + total[8:]

    def v_copy(k):
        return remote(
            v_out, v_all.at[slot, c], v_send.at[k], v_recv.at[slot * nc + c], ((r + k) % nr, home, l)
        )

    @pl.when(at_home)
    def _():
        v_all[slot, c] = v_out[...]

    @pl.when(jnp.logical_not(at_home))
    def _():
        v_copy(0).start()

    for k in range(1, nr):
        v_copy(k).start()

    pack_copy.wait_recv()
    y_first = (c * nl + l) * SY
    y_count = nc * nl * SY
    for g, ref in ((0, pack), (1, pack_in)):
        rate = ref[0:1, :] * (-STEP_SQ)

        def profile(t):
            value = jnp.exp(rate * (t - 7.5) * (t - 7.5))
            return jnp.where((t >= 0.0) & (t < float(TILE)), value, 0.0)

        tx = lax.broadcasted_iota(jnp.int32, (SX, rows), 0).astype(F32) + float(g * SX) - ref[1:2, :]
        ty = (lax.broadcasted_iota(jnp.int32, (SY, rows), 0) + y_first).astype(F32) - ref[2:3, :]
        ty = jnp.where(ty < 0.0, ty + float(y_count), ty)
        tz = lax.broadcasted_iota(jnp.int32, (GZ, rows), 0).astype(F32) - ref[3:4, :]
        tz = jnp.where(tz < 0.0, tz + float(GZ), tz)
        px, py = profile(tx), profile(ty)
        for x in range(SX):
            shape_xy[g, x * SY : (x + 1) * SY, :] = (px[x : x + 1, :] * py).astype(BF16)
        shape_z[g] = profile(tz)

    def direct(i):
        return (c * ratio + i) % 2 == r % 2

    def fwd_copy(i, cc, h):
        return remote(
            piece(i, cc, h), piece(i, cc, h), fwd_send.at[sem_at(i, cc, h)],
            piece_recv.at[sem_at(i, cc, h)], (sibling, c, l),
        )

    def landed(i, cc, h):
        fwd_copy(i, cc, h).wait_recv()

    for h in range(IN_CHUNKS):
        for i in range(ratio):
            for k in range(nc):
                cc = (c + 1 + k) % nc

                @pl.when(direct(i))
                def _():
                    mine = (c * ratio + i == r) & (cc == c)

                    @pl.when(mine)
                    def _():
                        own_copy(h).wait()

                    @pl.when(jnp.logical_not(mine))
                    def _():
                        landed(i, cc, h)

                    fwd_copy(i, cc, h).start()

    for i in range(ratio):
        for cc in range(nc):

            @pl.when(jnp.logical_not((c * ratio + i == r) & (cc == c)))
            def _():
                remote(v_out, v_all.at[i, cc], v_send.at[0], v_recv.at[i * nc + cc], (r, c, l)).wait_recv()

    total = jnp.zeros((16, rows), F32)
    for i in range(ratio):
        v = v_all[i, 0]
        for cc in range(1, nc):
            v = v + v_all[i, cc]
        total = total + dot_nt(hi_lo(v), m_buf[:, i * rows : (i + 1) * rows])
    q_out[...] = total[:8] + total[8:]
    q_all[0, c] = q_out[...]

    def q_copy(g, k):
        return remote(
            q_out, q_all.at[g, c], q_send.at[g * nc + k], q_recv.at[g * nc + k],
            ((r + g) % nr, (c + k) % nc, l),
        )

    sent_q = [(g, k) for g in range(2) for k in range(nc) if g or k]
    for g, k in sent_q:
        q_copy(g, k).start()

    for h in range(IN_CHUNKS):
        for i in range(ratio):
            for k in range(nc):

                @pl.when(jnp.logical_not(direct(i)))
                def _():
                    landed(i, (c + 1 + k) % nc, h)

    tall = rows // OUT_CHUNKS

    def product(cc, o):
        at = pl.ds(o * tall, tall)
        total = jnp.dot(m_buf[at, 0:rows], right[0, cc], preferred_element_type=F32)
        for i in range(1, ratio):
            total = total + jnp.dot(
                m_buf[at, i * rows : (i + 1) * rows], right[i, cc], preferred_element_type=F32
            )
        return total

    def part_copy(k, o):
        at = pl.ds(o * tall, tall)
        index = (k - 1) * OUT_CHUNKS + o
        return remote(
            part_out.at[k - 1, at, :], part_in.at[k - 1, at, :], part_send.at[index],
            part_recv.at[index], (r, (c + k) % nc, l),
        )

    for k in range(1, nc):
        for o in range(OUT_CHUNKS):
            part_out[k - 1, o * tall : (o + 1) * tall, :] = product((c + k) % nc, o).astype(BF16)
            part_copy(k, o).start()

    for g, k in sent_q:
        q_copy(g, k).wait_recv()
    total = jnp.zeros((SX * SY, GZ), F32)
    for g in range(2):
        charge = q_all[g, 0]
        for cc in range(1, nc):
            charge = charge + q_all[g, cc]
        total = total + dot_nt(shape_xy[g], (shape_z[g] * charge[0:1, :]).astype(BF16))
    den_ref[...] = total.reshape(SX, SY, GZ)

    for o in range(OUT_CHUNKS):
        total = product(c, o)
        for k in range(1, nc):
            part_copy(k, o).wait_recv()
            total = total + part_in[k - 1, o * tall : (o + 1) * tall, :].astype(F32)
        sq_ref[o * tall : (o + 1) * tall, :] = total.astype(BF16)

    for copy in w_copies:
        copy.wait_send()
    pack_copy.wait_send()
    for k in range(1, nr):
        v_copy(k).wait_send()
    for g, k in sent_q:
        q_copy(g, k).wait_send()
    for h in range(IN_CHUNKS):
        for k in range(1, nr // 2):
            piece_copy(k, h).wait_send()
        for i in range(ratio):
            for cc in range(nc):

                @pl.when(direct(i))
                def _():
                    fwd_copy(i, cc, h).wait_send()

    @pl.when(jnp.logical_not(at_home))
    def _():
        v_copy(0).wait_send()
        for h in range(IN_CHUNKS):
            piece_copy(0, h).wait_send()

    for k in range(1, nc):
        for o in range(OUT_CHUNKS):
            part_copy(k, o).wait_send()


def local(sizes, density_matrix, block_mask, weights, exponents, anchor_x, anchor_y, anchor_z):
    nr, nc, nl = sizes
    ratio = nr // nc
    rows, cols = density_matrix.shape
    width = cols // nl
    dma = pltpu.SemaphoreType.DMA
    pieces = ratio * nc * IN_CHUNKS
    vmem = pl.BlockSpec(memory_space=pltpu.VMEM)
    smem = pl.BlockSpec(memory_space=pltpu.SMEM)
    return pl.pallas_call(
        functools.partial(kernel, sizes),
        out_shape=(
            jax.ShapeDtypeStruct((rows, width), BF16),
            jax.ShapeDtypeStruct((SX, SY, GZ), F32),
        ),
        in_specs=[vmem] * 4 + [smem] * 3,
        out_specs=(vmem, vmem),
        scratch_shapes=[
            pltpu.VMEM((rows, cols), BF16),
            pltpu.VMEM((ratio, nc, rows, width), BF16),
            pltpu.VMEM((nc - 1, rows, width), BF16),
            pltpu.VMEM((nc - 1, rows, width), BF16),
            pltpu.VMEM((nl, 8, width), F32),
            pltpu.VMEM((8, rows), F32),
            pltpu.VMEM((ratio, nc, 8, rows), F32),
            pltpu.VMEM((8, rows), F32),
            pltpu.VMEM((2, nc, 8, rows), F32),
            pltpu.VMEM((8, rows), F32),
            pltpu.VMEM((8, rows), F32),
            pltpu.VMEM((2, SX * SY, rows), BF16),
            pltpu.VMEM((2, GZ, rows), F32),
            dma((nr // 2 * IN_CHUNKS,)),
            dma((pieces,)),
            dma((pieces,)),
            dma(((nc - 1) * OUT_CHUNKS,)),
            dma(((nc - 1) * OUT_CHUNKS,)),
            dma((nl - 1,)),
            dma((nl - 1,)),
            dma((nr,)),
            dma((ratio * nc,)),
            dma((2 * nc,)),
            dma((2 * nc,)),
            dma((1,)),
            dma((1,)),
        ],
        compiler_params=pltpu.CompilerParams(
            collective_id=0, has_side_effects=True, vmem_limit_bytes=48 * 1024 * 1024
        ),
        name="square_collocate",
    )(
        density_matrix, block_mask, weights.reshape(1, -1), exponents.reshape(1, -1),
        anchor_x, anchor_y, anchor_z,
    )


def solution(mesh):
    sizes = (mesh.shape["row"], mesh.shape["col"], mesh.shape["layer"])
    return jax.shard_map(
        functools.partial(local, sizes),
        mesh=mesh,
        in_specs=(
            P("row", "col"), P("row", "col"), P(("col", "layer")),
            P("row"), P("row"), P("row"), P("row"),
        ),
        out_specs=(P("row", ("col", "layer")), P("row", ("col", "layer"), None)),
        check_vma=False,
    )
```

```python
import functools

import jax
import jax.numpy as jnp
from jax import lax
from jax.experimental import pallas as pl
from jax.experimental.pallas import tpu as pltpu
from jax.sharding import PartitionSpec as P

BLOCK = 64
TILE = 16
SX = 32
SY = 16
GZ = 128
STEP_SQ = 0.0625
MESH = pl.DeviceIdType.MESH
F32 = jnp.float32
BF16 = jnp.bfloat16
LANES = 128
OUT_CHUNKS = 2
LOADS = 2


def dot_nt(a, b):
    return lax.dot_general(a, b, (((1,), (1,)), ((), ())), preferred_element_type=F32)


def hi_lo(x):
    high = x.astype(BF16).astype(F32)
    return jnp.concatenate([high, x - high], axis=0).astype(BF16)


def kernel(
    sizes,
    a_hbm, mask_hbm, w_hbm, e_hbm, ax_hbm, ay_hbm, az_hbm,
    sq_ref, den_ref,
    a_ref, mask_ref, w_ref, e_ref, ax_ref, ay_ref, az_ref, load_sem,
    m_buf, right, part_out, part_in, w_all, v_out, v_all, q_out, q_all, pack, pack_in, shape_xy, shape_low, shape_z,
    piece_send, piece_recv, fwd_send, part_send, part_recv,
    w_send, w_recv, v_send, v_recv, q_send, q_recv, pack_send, pack_recv,
):
    nr, nc, nl = sizes
    ratio = nr // nc
    rows, cols = a_ref.shape
    width = cols // nl
    atoms = rows // BLOCK
    r, c, l = lax.axis_index("row"), lax.axis_index("col"), lax.axis_index("layer")
    sibling = r + 1 - 2 * (r % 2)
    following = (r + 1) % nr

    def remote(src, dst, send, recv, device):
        return pltpu.make_async_remote_copy(
            src_ref=src, dst_ref=dst, send_sem=send, recv_sem=recv,
            device_id=device, device_id_type=MESH,
        )

    chunks = width // LANES
    tall = rows // LOADS
    small = [
        pltpu.make_async_copy(src, dst, load_sem.at[at])
        for at, (src, dst) in enumerate((
            (mask_hbm, mask_ref), (w_hbm, w_ref), (e_hbm, e_ref),
            (ax_hbm, ax_ref), (ay_hbm, ay_ref), (az_hbm, az_ref),
        ))
    ]
    large = [
        pltpu.make_async_copy(
            a_hbm.at[pl.ds(p * tall, tall), :], a_ref.at[pl.ds(p * tall, tall), :], load_sem.at[6 + p]
        )
        for p in range(LOADS)
    ]
    for copy in small + large:
        copy.start()

    barrier = pltpu.get_barrier_semaphore()
    peers = 0
    for dr in range(nr):
        for dc in range(nc):
            if dr or dc:
                peers += 1
                pl.semaphore_signal(
                    barrier, inc=1, device_id=((r + dr) % nr, (c + dc) % nc, l), device_id_type=MESH
                )
    for k in range(1, nl):
        peers += 1
        pl.semaphore_signal(barrier, inc=1, device_id=(r, c, (l + k) % nl), device_id_type=MESH)

    for copy in small:
        copy.wait()
    kept = jnp.where(mask_ref[...] > 0, 1.0, 0.0).astype(F32)
    spread = lax.broadcasted_iota(jnp.int32, (cols // BLOCK, cols), 1) // BLOCK
    pick = lax.broadcasted_iota(jnp.int32, (cols // BLOCK, cols), 0)
    wide = jnp.dot(kept, jnp.where(spread == pick, 1.0, 0.0).astype(F32), preferred_element_type=F32)
    w_all[l] = jnp.broadcast_to(w_ref[...], (8, width))
    lane_atom = lax.broadcasted_iota(jnp.int32, (8, rows), 1) // BLOCK
    sub = lax.broadcasted_iota(jnp.int32, (8, rows), 0)
    table = jnp.broadcast_to(e_ref[...], (8, rows))
    for j in range(atoms):
        here = lane_atom == j
        for at, ref in ((1, ax_ref), (2, ay_ref), (3, az_ref)):
            table = jnp.where(here & (sub == at), ref[j].astype(F32), table)
    pack[...] = table
    for b in range(atoms):
        if b % (atoms // LOADS) == 0:
            large[b // (atoms // LOADS)].wait()
        at = pl.ds(b * BLOCK, BLOCK)
        m_buf[at, :] = a_ref[at, :] * jnp.broadcast_to(wide[b : b + 1, :], (BLOCK, cols)).astype(BF16)

    pl.semaphore_wait(barrier, peers)

    w_copies = [
        remote(w_all.at[l], w_all.at[l], w_send.at[k - 1], w_recv.at[k - 1], (r, c, (l + k) % nl))
        for k in range(1, nl)
    ]
    for copy in w_copies:
        copy.start()
    pack_copy = remote(pack, pack_in, pack_send.at[0], pack_recv.at[0], (following, c, l))
    pack_copy.start()

    home = r // ratio
    slot = r % ratio

    def strip(h):
        return m_buf.at[:, pl.ds(pl.multiple_of(l * width + h * LANES, LANES), LANES)]

    def piece(i, cc, h):
        return right.at[i, cc, h]

    def sem_at(i, cc, h):
        return (i * nc + cc) * chunks + h

    def piece_copy(k, h):
        return remote(
            strip(h), piece(slot, c, h), piece_send.at[k * chunks + h],
            piece_recv.at[sem_at(slot, c, h)], ((r + 2 * k) % nr, home, l),
        )

    def own_copy(h):
        return pltpu.make_async_copy(strip(h), piece(slot, c, h), piece_recv.at[sem_at(slot, c, h)])

    at_home = home == c
    for h in range(chunks):
        for k in range(1, nr // 2):
            piece_copy(k, h).start()

        @pl.when(at_home)
        def _():
            own_copy(h).start()

        @pl.when(jnp.logical_not(at_home))
        def _():
            piece_copy(0, h).start()

    y_first = (c * nl + l) * SY
    y_count = nc * nl * SY

    def profiles(g, ref):
        rate = ref[0:1, :] * (-STEP_SQ)

        def profile(t):
            value = jnp.exp(rate * (t - 7.5) * (t - 7.5))
            return jnp.where((t >= 0.0) & (t < float(TILE)), value, 0.0)

        tx = lax.broadcasted_iota(jnp.int32, (SX, rows), 0).astype(F32) + float(g * SX) - ref[1:2, :]
        ty = (lax.broadcasted_iota(jnp.int32, (SY, rows), 0) + y_first).astype(F32) - ref[2:3, :]
        ty = jnp.where(ty < 0.0, ty + float(y_count), ty)
        tz = lax.broadcasted_iota(jnp.int32, (GZ, rows), 0).astype(F32) - ref[3:4, :]
        tz = jnp.where(tz < 0.0, tz + float(GZ), tz)
        px, py = profile(tx), profile(ty)
        for x in range(SX):
            plane = px[x : x + 1, :] * py
            high = plane.astype(BF16)
            shape_xy[g, x * SY : (x + 1) * SY, :] = high
            shape_low[g, x * SY : (x + 1) * SY, :] = (plane - high.astype(F32)).astype(BF16)
        shape_z[g] = profile(tz)

    profiles(0, pack)

    for copy in w_copies:
        copy.wait_recv()
    total = jnp.zeros((16, rows), F32)
    for k in range(nl):
        total = total + dot_nt(hi_lo(w_all[k]), m_buf[:, k * width : (k + 1) * width])
    v_out[...] = total[:8] + total[8:]

    def v_copy(k):
        return remote(
            v_out, v_all.at[slot, c], v_send.at[k], v_recv.at[slot * nc + c], ((r + k) % nr, home, l)
        )

    @pl.when(at_home)
    def _():
        v_all[slot, c] = v_out[...]

    @pl.when(jnp.logical_not(at_home))
    def _():
        v_copy(0).start()

    for k in range(1, nr):
        v_copy(k).start()

    pack_copy.wait_recv()
    profiles(1, pack_in)

    def direct(i):
        return (c * ratio + i) % 2 == r % 2

    def fwd_copy(i, cc, h):
        return remote(
            piece(i, cc, h), piece(i, cc, h), fwd_send.at[sem_at(i, cc, h)],
            piece_recv.at[sem_at(i, cc, h)], (sibling, c, l),
        )

    def landed(i, cc, h):
        fwd_copy(i, cc, h).wait_recv()

    def pass_on(h):
        for k in range(nc):
            cc = (c + 1 + k) % nc
            for i in range(ratio):

                @pl.when(direct(i))
                def _():
                    mine = (c * ratio + i == r) & (cc == c)

                    @pl.when(mine)
                    def _():
                        own_copy(h).wait()

                    @pl.when(jnp.logical_not(mine))
                    def _():
                        landed(i, cc, h)

                    fwd_copy(i, cc, h).start()

    def take(cc, h):
        for i in range(ratio):

            @pl.when(jnp.logical_not(direct(i)))
            def _():
                landed(i, cc, h)

    low = rows // OUT_CHUNKS

    def product(cc, h, at):
        total = jnp.dot(m_buf[at, 0:rows], right[0, cc, h], preferred_element_type=F32)
        for i in range(1, ratio):
            total = total + jnp.dot(
                m_buf[at, i * rows : (i + 1) * rows], right[i, cc, h], preferred_element_type=F32
            )
        return total

    def part_copy(k, h, o):
        at = pl.ds(o * low, low)
        index = ((k - 1) * chunks + h) * OUT_CHUNKS + o
        return remote(
            part_out.at[k - 1, h, at, :], part_in.at[k - 1, h, at, :], part_send.at[index],
            part_recv.at[index], (r, (c + k) % nc, l),
        )

    def parts(h):
        for k in range(1, nc):
            take((c + k) % nc, h)
            for o in range(OUT_CHUNKS):
                at = pl.ds(o * low, low)
                part_out[k - 1, h, at, :] = product((c + k) % nc, h, at).astype(BF16)
                part_copy(k, h, o).start()

    def charge_share():
        for i in range(ratio):
            for cc in range(nc):

                @pl.when(jnp.logical_not((c * ratio + i == r) & (cc == c)))
                def _():
                    remote(
                        v_out, v_all.at[i, cc], v_send.at[0], v_recv.at[i * nc + cc], (r, c, l)
                    ).wait_recv()

        total = jnp.zeros((16, rows), F32)
        for i in range(ratio):
            v = v_all[i, 0]
            for cc in range(1, nc):
                v = v + v_all[i, cc]
            total = total + dot_nt(hi_lo(v), m_buf[:, i * rows : (i + 1) * rows])
        q_out[...] = total[:8] + total[8:]
        q_all[0, c] = q_out[...]

    def q_copy(g, k):
        return remote(
            q_out, q_all.at[g, c], q_send.at[g * nc + k], q_recv.at[g * nc + k],
            ((r + g) % nr, (c + k) % nc, l),
        )

    sent_q = [(g, k) for g in range(2) for k in range(nc) if g or k]
    for h in range(chunks):
        pass_on(h)
        if h == chunks - 1:
            charge_share()
            for g, k in sent_q:
                q_copy(g, k).start()
        parts(h)

    for g, k in sent_q:
        q_copy(g, k).wait_recv()
    total = jnp.zeros((SX * SY, GZ), F32)
    for g in range(2):
        charge = q_all[g, 0]
        for cc in range(1, nc):
            charge = charge + q_all[g, cc]
        value = shape_z[g] * charge[0:1, :]
        high = value.astype(BF16)
        rest = (value - high.astype(F32)).astype(BF16)
        total = total + dot_nt(shape_xy[g], high) + dot_nt(shape_xy[g], rest) + dot_nt(shape_low[g], high)
    den_ref[...] = total.reshape(SX, SY, GZ)

    for h in range(chunks):
        take(c, h)
        for o in range(OUT_CHUNKS):
            at = pl.ds(o * low, low)
            total = product(c, h, at)
            for k in range(1, nc):
                part_copy(k, h, o).wait_recv()
                total = total + part_in[k - 1, h, at, :].astype(F32)
            sq_ref[at, h * LANES : (h + 1) * LANES] = total.astype(BF16)

    for copy in w_copies:
        copy.wait_send()
    pack_copy.wait_send()
    for k in range(1, nr):
        v_copy(k).wait_send()
    for g, k in sent_q:
        q_copy(g, k).wait_send()
    for h in range(chunks):
        for k in range(1, nr // 2):
            piece_copy(k, h).wait_send()
        for i in range(ratio):
            for cc in range(nc):

                @pl.when(direct(i))
                def _():
                    fwd_copy(i, cc, h).wait_send()

    @pl.when(jnp.logical_not(at_home))
    def _():
        v_copy(0).wait_send()
        for h in range(chunks):
            piece_copy(0, h).wait_send()

    for k in range(1, nc):
        for h in range(chunks):
            for o in range(OUT_CHUNKS):
                part_copy(k, h, o).wait_send()


def local(sizes, density_matrix, block_mask, weights, exponents, anchor_x, anchor_y, anchor_z):
    nr, nc, nl = sizes
    ratio = nr // nc
    rows, cols = density_matrix.shape
    width = cols // nl
    dma = pltpu.SemaphoreType.DMA
    chunks = width // LANES
    pieces = ratio * nc * chunks
    outs = (nc - 1) * chunks * OUT_CHUNKS
    hbm = pl.BlockSpec(memory_space=pltpu.HBM)
    vmem = pl.BlockSpec(memory_space=pltpu.VMEM)
    return pl.pallas_call(
        functools.partial(kernel, sizes),
        out_shape=(
            jax.ShapeDtypeStruct((rows, width), BF16),
            jax.ShapeDtypeStruct((SX, SY, GZ), F32),
        ),
        in_specs=[hbm] * 7,
        out_specs=(vmem, vmem),
        scratch_shapes=[
            pltpu.VMEM((rows, cols), BF16),
            pltpu.VMEM(block_mask.shape, jnp.int32),
            pltpu.VMEM((1, width), F32),
            pltpu.VMEM((1, rows), F32),
            pltpu.SMEM(anchor_x.shape, jnp.int32),
            pltpu.SMEM(anchor_x.shape, jnp.int32),
            pltpu.SMEM(anchor_x.shape, jnp.int32),
            dma((6 + LOADS,)),
            pltpu.VMEM((rows, cols), BF16),
            pltpu.VMEM((ratio, nc, chunks, rows, LANES), BF16),
            pltpu.VMEM((nc - 1, chunks, rows, LANES), BF16),
            pltpu.VMEM((nc - 1, chunks, rows, LANES), BF16),
            pltpu.VMEM((nl, 8, width), F32),
            pltpu.VMEM((8, rows), F32),
            pltpu.VMEM((ratio, nc, 8, rows), F32),
            pltpu.VMEM((8, rows), F32),
            pltpu.VMEM((2, nc, 8, rows), F32),
            pltpu.VMEM((8, rows), F32),
            pltpu.VMEM((8, rows), F32),
            pltpu.VMEM((2, SX * SY, rows), BF16),
            pltpu.VMEM((2, SX * SY, rows), BF16),
            pltpu.VMEM((2, GZ, rows), F32),
            dma((nr // 2 * chunks,)),
            dma((pieces,)),
            dma((pieces,)),
            dma((outs,)),
            dma((outs,)),
            dma((nl - 1,)),
            dma((nl - 1,)),
            dma((nr,)),
            dma((ratio * nc,)),
            dma((2 * nc,)),
            dma((2 * nc,)),
            dma((1,)),
            dma((1,)),
        ],
        compiler_params=pltpu.CompilerParams(
            collective_id=0, has_side_effects=True, vmem_limit_bytes=67_043_328
        ),
        name="square_collocate",
    )(
        density_matrix, block_mask, weights.reshape(1, -1), exponents.reshape(1, -1),
        anchor_x, anchor_y, anchor_z,
    )


def solution(mesh):
    sizes = (mesh.shape["row"], mesh.shape["col"], mesh.shape["layer"])
    return jax.shard_map(
        functools.partial(local, sizes),
        mesh=mesh,
        in_specs=(
            P("row", "col"), P("row", "col"), P(("col", "layer")),
            P("row"), P("row"), P("row"), P("row"),
        ),
        out_specs=(P("row", ("col", "layer")), P("row", ("col", "layer"), None)),
        check_vma=False,
    )
```

```python
import functools

import jax
import jax.numpy as jnp
from jax import lax
from jax.experimental import pallas as pl
from jax.experimental.pallas import tpu as pltpu
from jax.sharding import PartitionSpec as P

BLOCK = 64
TILE = 16
SX = 32
SY = 16
GZ = 128
STEP_SQ = 0.0625
MESH = pl.DeviceIdType.MESH
F32 = jnp.float32
BF16 = jnp.bfloat16
LANES = 128
OUT_CHUNKS = 2
LOADS = 2


def dot_nt(a, b):
    return lax.dot_general(a, b, (((1,), (1,)), ((), ())), preferred_element_type=F32)


def hi_lo(x):
    high = x.astype(BF16).astype(F32)
    return jnp.concatenate([high, x - high], axis=0).astype(BF16)


def kernel(
    sizes,
    a_hbm, mask_hbm, w_hbm, e_hbm, ax_hbm, ay_hbm, az_hbm,
    sq_ref, den_ref,
    a_ref, mask_ref, w_ref, e_ref, ax_ref, ay_ref, az_ref, load_sem,
    m_buf, right, part_out, part_in, w_all, v_out, v_all, q_out, q_all, pack, pack_in, shape_xy, shape_low, shape_z,
    piece_send, piece_recv, fwd_send, part_send, part_recv,
    w_send, w_recv, v_send, v_recv, q_send, q_recv, pack_send, pack_recv,
):
    nr, nc, nl = sizes
    ratio = nr // nc
    rows, cols = a_ref.shape
    width = cols // nl
    atoms = rows // BLOCK
    r, c, l = lax.axis_index("row"), lax.axis_index("col"), lax.axis_index("layer")
    sibling = r + 1 - 2 * (r % 2)
    following = (r + 1) % nr

    def remote(src, dst, send, recv, device):
        return pltpu.make_async_remote_copy(
            src_ref=src, dst_ref=dst, send_sem=send, recv_sem=recv,
            device_id=device, device_id_type=MESH,
        )

    chunks = width // LANES
    tall = rows // LOADS
    small = [
        pltpu.make_async_copy(src, dst, load_sem.at[at])
        for at, (src, dst) in enumerate((
            (mask_hbm, mask_ref), (w_hbm, w_ref), (e_hbm, e_ref),
            (ax_hbm, ax_ref), (ay_hbm, ay_ref), (az_hbm, az_ref),
        ))
    ]
    large = [
        pltpu.make_async_copy(
            a_hbm.at[pl.ds(p * tall, tall), :], a_ref.at[pl.ds(p * tall, tall), :], load_sem.at[6 + p]
        )
        for p in range(LOADS)
    ]
    for copy in small + large:
        copy.start()

    barrier = pltpu.get_barrier_semaphore()
    peers = 0
    for dr in range(nr):
        for dc in range(nc):
            if dr or dc:
                peers += 1
                pl.semaphore_signal(
                    barrier, inc=1, device_id=((r + dr) % nr, (c + dc) % nc, l), device_id_type=MESH
                )
    for k in range(1, nl):
        peers += 1
        pl.semaphore_signal(barrier, inc=1, device_id=(r, c, (l + k) % nl), device_id_type=MESH)

    for copy in small:
        copy.wait()
    kept = jnp.where(mask_ref[...] > 0, 1.0, 0.0).astype(F32)
    spread = lax.broadcasted_iota(jnp.int32, (cols // BLOCK, cols), 1) // BLOCK
    pick = lax.broadcasted_iota(jnp.int32, (cols // BLOCK, cols), 0)
    wide = jnp.dot(kept, jnp.where(spread == pick, 1.0, 0.0).astype(F32), preferred_element_type=F32)
    w_all[l] = jnp.broadcast_to(w_ref[...], (8, width))
    lane_atom = lax.broadcasted_iota(jnp.int32, (8, rows), 1) // BLOCK
    sub = lax.broadcasted_iota(jnp.int32, (8, rows), 0)
    table = jnp.broadcast_to(e_ref[...], (8, rows))
    for j in range(atoms):
        here = lane_atom == j
        for at, ref in ((1, ax_ref), (2, ay_ref), (3, az_ref)):
            table = jnp.where(here & (sub == at), ref[j].astype(F32), table)
    pack[...] = table
    for b in range(atoms):
        if b % (atoms // LOADS) == 0:
            large[b // (atoms // LOADS)].wait()
        at = pl.ds(b * BLOCK, BLOCK)
        m_buf[at, :] = a_ref[at, :] * jnp.broadcast_to(wide[b : b + 1, :], (BLOCK, cols)).astype(BF16)

    pl.semaphore_wait(barrier, peers)

    w_copies = [
        remote(w_all.at[l], w_all.at[l], w_send.at[k - 1], w_recv.at[k - 1], (r, c, (l + k) % nl))
        for k in range(1, nl)
    ]
    for copy in w_copies:
        copy.start()
    pack_copy = remote(pack, pack_in, pack_send.at[0], pack_recv.at[0], (following, c, l))
    pack_copy.start()

    home = r // ratio
    slot = r % ratio

    def strip(h):
        return m_buf.at[:, pl.ds(pl.multiple_of(l * width + h * LANES, LANES), LANES)]

    def piece(i, cc, h):
        return right.at[i, cc, h]

    def sem_at(i, cc, h):
        return (i * nc + cc) * chunks + h

    def piece_copy(k, h):
        return remote(
            strip(h), piece(slot, c, h), piece_send.at[k * chunks + h],
            piece_recv.at[sem_at(slot, c, h)], ((r + 2 * k) % nr, home, l),
        )

    def own_copy(h):
        return pltpu.make_async_copy(strip(h), piece(slot, c, h), piece_recv.at[sem_at(slot, c, h)])

    at_home = home == c
    for h in range(chunks):
        for k in range(1, nr // 2):
            piece_copy(k, h).start()

        @pl.when(at_home)
        def _():
            own_copy(h).start()

        @pl.when(jnp.logical_not(at_home))
        def _():
            piece_copy(0, h).start()

    y_first = (c * nl + l) * SY
    y_count = nc * nl * SY

    def profiles(g, ref):
        rate = ref[0:1, :] * (-STEP_SQ)

        def profile(t):
            value = jnp.exp(rate * (t - 7.5) * (t - 7.5))
            return jnp.where((t >= 0.0) & (t < float(TILE)), value, 0.0)

        tx = lax.broadcasted_iota(jnp.int32, (SX, rows), 0).astype(F32) + float(g * SX) - ref[1:2, :]
        ty = (lax.broadcasted_iota(jnp.int32, (SY, rows), 0) + y_first).astype(F32) - ref[2:3, :]
        ty = jnp.where(ty < 0.0, ty + float(y_count), ty)
        tz = lax.broadcasted_iota(jnp.int32, (GZ, rows), 0).astype(F32) - ref[3:4, :]
        tz = jnp.where(tz < 0.0, tz + float(GZ), tz)
        px, py = profile(tx), profile(ty)
        for x in range(SX):
            plane = px[x : x + 1, :] * py
            high = plane.astype(BF16)
            shape_xy[g, x * SY : (x + 1) * SY, :] = high
            shape_low[g, x * SY : (x + 1) * SY, :] = (plane - high.astype(F32)).astype(BF16)
        shape_z[g] = profile(tz)

    profiles(0, pack)

    for copy in w_copies:
        copy.wait_recv()
    total = jnp.zeros((16, rows), F32)
    for k in range(nl):
        total = total + dot_nt(hi_lo(w_all[k]), m_buf[:, k * width : (k + 1) * width])
    v_out[...] = total[:8] + total[8:]

    def v_copy(k):
        return remote(
            v_out, v_all.at[slot, c], v_send.at[k], v_recv.at[slot * nc + c], ((r + k) % nr, home, l)
        )

    @pl.when(at_home)
    def _():
        v_all[slot, c] = v_out[...]

    @pl.when(jnp.logical_not(at_home))
    def _():
        v_copy(0).start()

    for k in range(1, nr):
        v_copy(k).start()

    pack_copy.wait_recv()
    profiles(1, pack_in)

    def direct(i):
        return (c * ratio + i) % 2 == r % 2

    def fwd_copy(i, cc, h):
        return remote(
            piece(i, cc, h), piece(i, cc, h), fwd_send.at[sem_at(i, cc, h)],
            piece_recv.at[sem_at(i, cc, h)], (sibling, c, l),
        )

    def landed(i, cc, h):
        fwd_copy(i, cc, h).wait_recv()

    def pass_on(h):
        for k in range(nc):
            cc = (c + 1 + k) % nc
            for i in range(ratio):

                @pl.when(direct(i))
                def _():
                    mine = (c * ratio + i == r) & (cc == c)

                    @pl.when(mine)
                    def _():
                        own_copy(h).wait()

                    @pl.when(jnp.logical_not(mine))
                    def _():
                        landed(i, cc, h)

                    fwd_copy(i, cc, h).start()

    def take(cc, h):
        for i in range(ratio):

            @pl.when(jnp.logical_not(direct(i)))
            def _():
                landed(i, cc, h)

    low = rows // OUT_CHUNKS

    def product(cc, h, at):
        total = jnp.dot(m_buf[at, 0:rows], right[0, cc, h], preferred_element_type=F32)
        for i in range(1, ratio):
            total = total + jnp.dot(
                m_buf[at, i * rows : (i + 1) * rows], right[i, cc, h], preferred_element_type=F32
            )
        return total

    def part_copy(k, h, o):
        at = pl.ds(o * low, low)
        index = ((k - 1) * chunks + h) * OUT_CHUNKS + o
        return remote(
            part_out.at[k - 1, h, at, :], part_in.at[k - 1, h, at, :], part_send.at[index],
            part_recv.at[index], (r, (c + k) % nc, l),
        )

    def parts(h):
        for k in range(1, nc):
            take((c + k) % nc, h)
            for o in range(OUT_CHUNKS):
                at = pl.ds(o * low, low)
                part_out[k - 1, h, at, :] = product((c + k) % nc, h, at).astype(BF16)
                part_copy(k, h, o).start()

    def charge_share():
        for i in range(ratio):
            for cc in range(nc):

                @pl.when(jnp.logical_not((c * ratio + i == r) & (cc == c)))
                def _():
                    remote(
                        v_out, v_all.at[i, cc], v_send.at[0], v_recv.at[i * nc + cc], (r, c, l)
                    ).wait_recv()

        total = jnp.zeros((16, rows), F32)
        for i in range(ratio):
            v = v_all[i, 0]
            for cc in range(1, nc):
                v = v + v_all[i, cc]
            total = total + dot_nt(hi_lo(v), m_buf[:, i * rows : (i + 1) * rows])
        q_out[...] = total[:8] + total[8:]
        q_all[0, c] = q_out[...]

    def q_copy(g, k):
        return remote(
            q_out, q_all.at[g, c], q_send.at[g * nc + k], q_recv.at[g * nc + k],
            ((r + g) % nr, (c + k) % nc, l),
        )

    sent_q = [(g, k) for g in range(2) for k in range(nc) if g or k]
    for h in range(chunks):
        pass_on(h)
        if h == chunks - 1:
            charge_share()
            for g, k in sent_q:
                q_copy(g, k).start()
        parts(h)

    for g, k in sent_q:
        q_copy(g, k).wait_recv()
    total = jnp.zeros((SX * SY, GZ), F32)
    for g in range(2):
        charge = q_all[g, 0]
        for cc in range(1, nc):
            charge = charge + q_all[g, cc]
        value = shape_z[g] * charge[0:1, :]
        high = value.astype(BF16)
        rest = (value - high.astype(F32)).astype(BF16)
        total = total + dot_nt(shape_xy[g], high) + dot_nt(shape_xy[g], rest) + dot_nt(shape_low[g], high)
    den_ref[...] = total.reshape(SX, SY, GZ)

    for h in range(chunks):
        take(c, h)
        for o in range(OUT_CHUNKS):
            at = pl.ds(o * low, low)
            total = product(c, h, at)
            for k in range(1, nc):
                part_copy(k, h, o).wait_recv()
                total = total + part_in[k - 1, h, at, :].astype(F32)
            sq_ref[at, h * LANES : (h + 1) * LANES] = total.astype(BF16)

    for copy in w_copies:
        copy.wait_send()
    pack_copy.wait_send()
    for k in range(1, nr):
        v_copy(k).wait_send()
    for g, k in sent_q:
        q_copy(g, k).wait_send()
    for h in range(chunks):
        for k in range(1, nr // 2):
            piece_copy(k, h).wait_send()
        for i in range(ratio):
            for cc in range(nc):

                @pl.when(direct(i))
                def _():
                    fwd_copy(i, cc, h).wait_send()

    @pl.when(jnp.logical_not(at_home))
    def _():
        v_copy(0).wait_send()
        for h in range(chunks):
            piece_copy(0, h).wait_send()

    for k in range(1, nc):
        for h in range(chunks):
            for o in range(OUT_CHUNKS):
                part_copy(k, h, o).wait_send()


def store(sq_ref, den_ref, sq_out, den_out, sem):
    copies = [
        pltpu.make_async_copy(sq_ref, sq_out, sem.at[0]),
        pltpu.make_async_copy(den_ref, den_out, sem.at[1]),
    ]
    for copy in copies:
        copy.start()
    for copy in copies:
        copy.wait()


def local(sizes, density_matrix, block_mask, weights, exponents, anchor_x, anchor_y, anchor_z):
    nr, nc, nl = sizes
    ratio = nr // nc
    rows, cols = density_matrix.shape
    width = cols // nl
    dma = pltpu.SemaphoreType.DMA
    chunks = width // LANES
    pieces = ratio * nc * chunks
    outs = (nc - 1) * chunks * OUT_CHUNKS
    hbm = pl.BlockSpec(memory_space=pltpu.HBM)
    vmem = pl.BlockSpec(memory_space=pltpu.VMEM)
    inputs = (
        density_matrix, block_mask, weights.reshape(1, -1), exponents.reshape(1, -1),
        anchor_x, anchor_y, anchor_z,
    )
    shapes = (
        jax.ShapeDtypeStruct((rows, width), BF16),
        jax.ShapeDtypeStruct((SX, SY, GZ), F32),
    )
    results = pl.pallas_call(
        functools.partial(kernel, sizes),
        out_shape=(pltpu.VMEM((rows, width), BF16), pltpu.VMEM((SX, SY, GZ), F32)),
        in_specs=[hbm] * 7,
        out_specs=(vmem, vmem),
        scratch_shapes=[
            pltpu.VMEM((rows, cols), BF16),
            pltpu.VMEM(block_mask.shape, jnp.int32),
            pltpu.VMEM((1, width), F32),
            pltpu.VMEM((1, rows), F32),
            pltpu.SMEM(anchor_x.shape, jnp.int32),
            pltpu.SMEM(anchor_x.shape, jnp.int32),
            pltpu.SMEM(anchor_x.shape, jnp.int32),
            dma((6 + LOADS,)),
            pltpu.VMEM((rows, cols), BF16),
            pltpu.VMEM((ratio, nc, chunks, rows, LANES), BF16),
            pltpu.VMEM((nc - 1, chunks, rows, LANES), BF16),
            pltpu.VMEM((nc - 1, chunks, rows, LANES), BF16),
            pltpu.VMEM((nl, 8, width), F32),
            pltpu.VMEM((8, rows), F32),
            pltpu.VMEM((ratio, nc, 8, rows), F32),
            pltpu.VMEM((8, rows), F32),
            pltpu.VMEM((2, nc, 8, rows), F32),
            pltpu.VMEM((8, rows), F32),
            pltpu.VMEM((8, rows), F32),
            pltpu.VMEM((2, SX * SY, rows), BF16),
            pltpu.VMEM((2, SX * SY, rows), BF16),
            pltpu.VMEM((2, GZ, rows), F32),
            dma((nr // 2 * chunks,)),
            dma((pieces,)),
            dma((pieces,)),
            dma((outs,)),
            dma((outs,)),
            dma((nl - 1,)),
            dma((nl - 1,)),
            dma((nr,)),
            dma((ratio * nc,)),
            dma((2 * nc,)),
            dma((2 * nc,)),
            dma((1,)),
            dma((1,)),
        ],
        compiler_params=pltpu.CompilerParams(
            collective_id=0, has_side_effects=True, vmem_limit_bytes=66_000_000
        ),
        name="square_collocate",
    )(*[pltpu.with_memory_space_constraint(x, pltpu.HBM) for x in inputs])
    return pl.pallas_call(
        store,
        out_shape=shapes,
        in_specs=[vmem] * 2,
        out_specs=(hbm, hbm),
        scratch_shapes=[dma((2,))],
        compiler_params=pltpu.CompilerParams(vmem_limit_bytes=4 * 1024 * 1024),
        name="store",
    )(*results)


def solution(mesh):
    sizes = (mesh.shape["row"], mesh.shape["col"], mesh.shape["layer"])
    return jax.shard_map(
        functools.partial(local, sizes),
        mesh=mesh,
        in_specs=(
            P("row", "col"), P("row", "col"), P(("col", "layer")),
            P("row"), P("row"), P("row"), P("row"),
        ),
        out_specs=(P("row", ("col", "layer")), P("row", ("col", "layer"), None)),
        check_vma=False,
    )
```

```python
import functools

import jax
import jax.numpy as jnp
from jax import lax
from jax.experimental import pallas as pl
from jax.experimental.pallas import tpu as pltpu
from jax.sharding import PartitionSpec as P

BLOCK = 64
TILE = 16
SX = 32
SY = 16
GZ = 128
STEP_SQ = 0.0625
MESH = pl.DeviceIdType.MESH
F32 = jnp.float32
BF16 = jnp.bfloat16
LANES = 128
OUT_CHUNKS = 2
LOADS = 2


def dot_nt(a, b):
    return lax.dot_general(a, b, (((1,), (1,)), ((), ())), preferred_element_type=F32)


def hi_lo(x):
    high = x.astype(BF16).astype(F32)
    return jnp.concatenate([high, x - high], axis=0).astype(BF16)


def kernel(
    sizes,
    a_hbm, mask_hbm, w_hbm, e_hbm, ax_hbm, ay_hbm, az_hbm,
    sq_ref, den_ref,
    a_ref, mask_ref, w_ref, e_ref, ax_ref, ay_ref, az_ref, load_sem,
    m_buf, right, own_part, part_out, part_in, w_all, v_out, v_all, q_out, q_all, pack, pack_in, shape_xy, shape_low, shape_z,
    piece_send, piece_recv, fwd_send, part_send, part_recv,
    w_send, w_recv, v_send, v_recv, q_send, q_recv, pack_send, pack_recv,
):
    nr, nc, nl = sizes
    ratio = nr // nc
    rows, cols = a_ref.shape
    width = cols // nl
    atoms = rows // BLOCK
    r, c, l = lax.axis_index("row"), lax.axis_index("col"), lax.axis_index("layer")
    sibling = r + 1 - 2 * (r % 2)
    following = (r + 1) % nr

    def remote(src, dst, send, recv, device):
        return pltpu.make_async_remote_copy(
            src_ref=src, dst_ref=dst, send_sem=send, recv_sem=recv,
            device_id=device, device_id_type=MESH,
        )

    chunks = width // LANES
    tall = rows // LOADS
    small = [
        pltpu.make_async_copy(src, dst, load_sem.at[at])
        for at, (src, dst) in enumerate((
            (mask_hbm, mask_ref), (w_hbm, w_ref), (e_hbm, e_ref),
            (ax_hbm, ax_ref), (ay_hbm, ay_ref), (az_hbm, az_ref),
        ))
    ]
    large = [
        pltpu.make_async_copy(
            a_hbm.at[pl.ds(p * tall, tall), :], a_ref.at[pl.ds(p * tall, tall), :], load_sem.at[6 + p]
        )
        for p in range(LOADS)
    ]
    for copy in small + large:
        copy.start()

    barrier = pltpu.get_barrier_semaphore()
    peers = 0
    for dr in range(nr):
        for dc in range(nc):
            if dr or dc:
                peers += 1
                pl.semaphore_signal(
                    barrier, inc=1, device_id=((r + dr) % nr, (c + dc) % nc, l), device_id_type=MESH
                )
    for k in range(1, nl):
        peers += 1
        pl.semaphore_signal(barrier, inc=1, device_id=(r, c, (l + k) % nl), device_id_type=MESH)

    for copy in small:
        copy.wait()
    kept = jnp.where(mask_ref[...] > 0, 1.0, 0.0).astype(F32)
    spread = lax.broadcasted_iota(jnp.int32, (cols // BLOCK, cols), 1) // BLOCK
    pick = lax.broadcasted_iota(jnp.int32, (cols // BLOCK, cols), 0)
    wide = jnp.dot(kept, jnp.where(spread == pick, 1.0, 0.0).astype(F32), preferred_element_type=F32)
    w_all[l] = jnp.broadcast_to(w_ref[...], (8, width))
    lane_atom = lax.broadcasted_iota(jnp.int32, (8, rows), 1) // BLOCK
    sub = lax.broadcasted_iota(jnp.int32, (8, rows), 0)
    table = jnp.broadcast_to(e_ref[...], (8, rows))
    for j in range(atoms):
        here = lane_atom == j
        for at, ref in ((1, ax_ref), (2, ay_ref), (3, az_ref)):
            table = jnp.where(here & (sub == at), ref[j].astype(F32), table)
    pack[...] = table
    for b in range(atoms):
        if b % (atoms // LOADS) == 0:
            large[b // (atoms // LOADS)].wait()
        at = pl.ds(b * BLOCK, BLOCK)
        m_buf[at, :] = a_ref[at, :] * jnp.broadcast_to(wide[b : b + 1, :], (BLOCK, cols)).astype(BF16)

    pl.semaphore_wait(barrier, peers)

    w_copies = [
        remote(w_all.at[l], w_all.at[l], w_send.at[k - 1], w_recv.at[k - 1], (r, c, (l + k) % nl))
        for k in range(1, nl)
    ]
    for copy in w_copies:
        copy.start()
    pack_copy = remote(pack, pack_in, pack_send.at[0], pack_recv.at[0], (following, c, l))
    pack_copy.start()

    home = r // ratio
    slot = r % ratio

    def strip(h):
        return m_buf.at[:, pl.ds(pl.multiple_of(l * width + h * LANES, LANES), LANES)]

    def piece(i, cc, h):
        return right.at[i, cc, h]

    def sem_at(i, cc, h):
        return (i * nc + cc) * chunks + h

    def piece_copy(k, h):
        return remote(
            strip(h), piece(slot, c, h), piece_send.at[k * chunks + h],
            piece_recv.at[sem_at(slot, c, h)], ((r + 2 * k) % nr, home, l),
        )

    def own_copy(h):
        return pltpu.make_async_copy(strip(h), piece(slot, c, h), piece_recv.at[sem_at(slot, c, h)])

    at_home = home == c
    for h in range(chunks):
        for k in range(1, nr // 2):
            piece_copy(k, h).start()

        @pl.when(at_home)
        def _():
            own_copy(h).start()

        @pl.when(jnp.logical_not(at_home))
        def _():
            piece_copy(0, h).start()

    y_first = (c * nl + l) * SY
    y_count = nc * nl * SY

    def profiles(g, ref):
        rate = ref[0:1, :] * (-STEP_SQ)

        def profile(t):
            value = jnp.exp(rate * (t - 7.5) * (t - 7.5))
            return jnp.where((t >= 0.0) & (t < float(TILE)), value, 0.0)

        tx = lax.broadcasted_iota(jnp.int32, (SX, rows), 0).astype(F32) + float(g * SX) - ref[1:2, :]
        ty = (lax.broadcasted_iota(jnp.int32, (SY, rows), 0) + y_first).astype(F32) - ref[2:3, :]
        ty = jnp.where(ty < 0.0, ty + float(y_count), ty)
        tz = lax.broadcasted_iota(jnp.int32, (GZ, rows), 0).astype(F32) - ref[3:4, :]
        tz = jnp.where(tz < 0.0, tz + float(GZ), tz)
        px, py = profile(tx), profile(ty)
        for x in range(SX):
            plane = px[x : x + 1, :] * py
            high = plane.astype(BF16)
            shape_xy[g, x * SY : (x + 1) * SY, :] = high
            shape_low[g, x * SY : (x + 1) * SY, :] = (plane - high.astype(F32)).astype(BF16)
        shape_z[g] = profile(tz)

    profiles(0, pack)

    for copy in w_copies:
        copy.wait_recv()
    total = jnp.zeros((16, rows), F32)
    for k in range(nl):
        total = total + dot_nt(hi_lo(w_all[k]), m_buf[:, k * width : (k + 1) * width])
    v_out[...] = total[:8] + total[8:]

    def v_copy(k):
        return remote(
            v_out, v_all.at[slot, c], v_send.at[k], v_recv.at[slot * nc + c], ((r + k) % nr, home, l)
        )

    @pl.when(at_home)
    def _():
        v_all[slot, c] = v_out[...]

    @pl.when(jnp.logical_not(at_home))
    def _():
        v_copy(0).start()

    for k in range(1, nr):
        v_copy(k).start()

    pack_copy.wait_recv()
    profiles(1, pack_in)

    def direct(i):
        return (c * ratio + i) % 2 == r % 2

    def fwd_copy(i, cc, h):
        return remote(
            piece(i, cc, h), piece(i, cc, h), fwd_send.at[sem_at(i, cc, h)],
            piece_recv.at[sem_at(i, cc, h)], (sibling, c, l),
        )

    def landed(i, cc, h):
        fwd_copy(i, cc, h).wait_recv()

    def pass_on(h):
        for k in range(nc):
            cc = (c + 1 + k) % nc
            for i in range(ratio):

                @pl.when(direct(i))
                def _():
                    mine = (c * ratio + i == r) & (cc == c)

                    @pl.when(mine)
                    def _():
                        own_copy(h).wait()

                    @pl.when(jnp.logical_not(mine))
                    def _():
                        landed(i, cc, h)

                    fwd_copy(i, cc, h).start()

    def take(cc, h):
        for i in range(ratio):

            @pl.when(jnp.logical_not(direct(i)))
            def _():
                landed(i, cc, h)

    low = rows // OUT_CHUNKS

    def product(cc, h, at):
        total = jnp.dot(m_buf[at, 0:rows], right[0, cc, h], preferred_element_type=F32)
        for i in range(1, ratio):
            total = total + jnp.dot(
                m_buf[at, i * rows : (i + 1) * rows], right[i, cc, h], preferred_element_type=F32
            )
        return total

    def part_copy(k, h, o):
        at = pl.ds(o * low, low)
        index = ((k - 1) * chunks + h) * OUT_CHUNKS + o
        return remote(
            part_out.at[k - 1, h, at, :], part_in.at[k - 1, h, at, :], part_send.at[index],
            part_recv.at[index], (r, (c + k) % nc, l),
        )

    def parts(h):
        for k in range(1, nc):
            take((c + k) % nc, h)
            for o in range(OUT_CHUNKS):
                at = pl.ds(o * low, low)
                part_out[k - 1, h, at, :] = product((c + k) % nc, h, at).astype(BF16)
                part_copy(k, h, o).start()

    def charge_share():
        for i in range(ratio):
            for cc in range(nc):

                @pl.when(jnp.logical_not((c * ratio + i == r) & (cc == c)))
                def _():
                    remote(
                        v_out, v_all.at[i, cc], v_send.at[0], v_recv.at[i * nc + cc], (r, c, l)
                    ).wait_recv()

        total = jnp.zeros((16, rows), F32)
        for i in range(ratio):
            v = v_all[i, 0]
            for cc in range(1, nc):
                v = v + v_all[i, cc]
            total = total + dot_nt(hi_lo(v), m_buf[:, i * rows : (i + 1) * rows])
        q_out[...] = total[:8] + total[8:]
        q_all[0, c] = q_out[...]

    def q_copy(g, k):
        return remote(
            q_out, q_all.at[g, c], q_send.at[g * nc + k], q_recv.at[g * nc + k],
            ((r + g) % nr, (c + k) % nc, l),
        )

    sent_q = [(g, k) for g in range(2) for k in range(nc) if g or k]
    for h in range(chunks):
        pass_on(h)
        if h == chunks - 1:
            charge_share()
            for g, k in sent_q:
                q_copy(g, k).start()
        parts(h)

    for h in range(chunks):
        take(c, h)
        for o in range(OUT_CHUNKS):
            at = pl.ds(o * low, low)
            own_part[h, at, :] = product(c, h, at)

    for g, k in sent_q:
        q_copy(g, k).wait_recv()
    total = jnp.zeros((SX * SY, GZ), F32)
    for g in range(2):
        charge = q_all[g, 0]
        for cc in range(1, nc):
            charge = charge + q_all[g, cc]
        value = shape_z[g] * charge[0:1, :]
        high = value.astype(BF16)
        rest = (value - high.astype(F32)).astype(BF16)
        total = total + dot_nt(shape_xy[g], high) + dot_nt(shape_xy[g], rest) + dot_nt(shape_low[g], high)
    den_ref[...] = total.reshape(SX, SY, GZ)

    for h in range(chunks):
        for o in range(OUT_CHUNKS):
            at = pl.ds(o * low, low)
            total = own_part[h, at, :]
            for k in range(1, nc):
                part_copy(k, h, o).wait_recv()
                total = total + part_in[k - 1, h, at, :].astype(F32)
            sq_ref[at, h * LANES : (h + 1) * LANES] = total.astype(BF16)

    for copy in w_copies:
        copy.wait_send()
    pack_copy.wait_send()
    for k in range(1, nr):
        v_copy(k).wait_send()
    for g, k in sent_q:
        q_copy(g, k).wait_send()
    for h in range(chunks):
        for k in range(1, nr // 2):
            piece_copy(k, h).wait_send()
        for i in range(ratio):
            for cc in range(nc):

                @pl.when(direct(i))
                def _():
                    fwd_copy(i, cc, h).wait_send()

    @pl.when(jnp.logical_not(at_home))
    def _():
        v_copy(0).wait_send()
        for h in range(chunks):
            piece_copy(0, h).wait_send()

    for k in range(1, nc):
        for h in range(chunks):
            for o in range(OUT_CHUNKS):
                part_copy(k, h, o).wait_send()


def store(sq_ref, den_ref, sq_out, den_out, sem):
    copies = [
        pltpu.make_async_copy(sq_ref, sq_out, sem.at[0]),
        pltpu.make_async_copy(den_ref, den_out, sem.at[1]),
    ]
    for copy in copies:
        copy.start()
    for copy in copies:
        copy.wait()


def local(sizes, density_matrix, block_mask, weights, exponents, anchor_x, anchor_y, anchor_z):
    nr, nc, nl = sizes
    ratio = nr // nc
    rows, cols = density_matrix.shape
    width = cols // nl
    dma = pltpu.SemaphoreType.DMA
    chunks = width // LANES
    pieces = ratio * nc * chunks
    outs = (nc - 1) * chunks * OUT_CHUNKS
    hbm = pl.BlockSpec(memory_space=pltpu.HBM)
    vmem = pl.BlockSpec(memory_space=pltpu.VMEM)
    inputs = (
        density_matrix, block_mask, weights.reshape(1, -1), exponents.reshape(1, -1),
        anchor_x, anchor_y, anchor_z,
    )
    shapes = (
        jax.ShapeDtypeStruct((rows, width), BF16),
        jax.ShapeDtypeStruct((SX, SY, GZ), F32),
    )
    results = pl.pallas_call(
        functools.partial(kernel, sizes),
        out_shape=(pltpu.VMEM((rows, width), BF16), pltpu.VMEM((SX, SY, GZ), F32)),
        in_specs=[hbm] * 7,
        out_specs=(vmem, vmem),
        scratch_shapes=[
            pltpu.VMEM((rows, cols), BF16),
            pltpu.VMEM(block_mask.shape, jnp.int32),
            pltpu.VMEM((1, width), F32),
            pltpu.VMEM((1, rows), F32),
            pltpu.SMEM(anchor_x.shape, jnp.int32),
            pltpu.SMEM(anchor_x.shape, jnp.int32),
            pltpu.SMEM(anchor_x.shape, jnp.int32),
            dma((6 + LOADS,)),
            pltpu.VMEM((rows, cols), BF16),
            pltpu.VMEM((ratio, nc, chunks, rows, LANES), BF16),
            pltpu.VMEM((chunks, rows, LANES), F32),
            pltpu.VMEM((nc - 1, chunks, rows, LANES), BF16),
            pltpu.VMEM((nc - 1, chunks, rows, LANES), BF16),
            pltpu.VMEM((nl, 8, width), F32),
            pltpu.VMEM((8, rows), F32),
            pltpu.VMEM((ratio, nc, 8, rows), F32),
            pltpu.VMEM((8, rows), F32),
            pltpu.VMEM((2, nc, 8, rows), F32),
            pltpu.VMEM((8, rows), F32),
            pltpu.VMEM((8, rows), F32),
            pltpu.VMEM((2, SX * SY, rows), BF16),
            pltpu.VMEM((2, SX * SY, rows), BF16),
            pltpu.VMEM((2, GZ, rows), F32),
            dma((nr // 2 * chunks,)),
            dma((pieces,)),
            dma((pieces,)),
            dma((outs,)),
            dma((outs,)),
            dma((nl - 1,)),
            dma((nl - 1,)),
            dma((nr,)),
            dma((ratio * nc,)),
            dma((2 * nc,)),
            dma((2 * nc,)),
            dma((1,)),
            dma((1,)),
        ],
        compiler_params=pltpu.CompilerParams(
            collective_id=0, has_side_effects=True, vmem_limit_bytes=66_000_000
        ),
        name="square_collocate",
    )(*[pltpu.with_memory_space_constraint(x, pltpu.HBM) for x in inputs])
    return pl.pallas_call(
        store,
        out_shape=shapes,
        in_specs=[vmem] * 2,
        out_specs=(hbm, hbm),
        scratch_shapes=[dma((2,))],
        compiler_params=pltpu.CompilerParams(vmem_limit_bytes=4 * 1024 * 1024),
        name="store",
    )(*results)


def solution(mesh):
    sizes = (mesh.shape["row"], mesh.shape["col"], mesh.shape["layer"])
    return jax.shard_map(
        functools.partial(local, sizes),
        mesh=mesh,
        in_specs=(
            P("row", "col"), P("row", "col"), P(("col", "layer")),
            P("row"), P("row"), P("row"), P("row"),
        ),
        out_specs=(P("row", ("col", "layer")), P("row", ("col", "layer"), None)),
        check_vma=False,
    )
```

```python
import functools

import jax
import jax.numpy as jnp
from jax import lax
from jax.experimental import pallas as pl
from jax.experimental.pallas import tpu as pltpu
from jax.sharding import PartitionSpec as P

BLOCK = 64
TILE = 16
SX = 32
SY = 16
GZ = 128
STEP_SQ = 0.0625
MESH = pl.DeviceIdType.MESH
F32 = jnp.float32
BF16 = jnp.bfloat16
LANES = 128
OUT_CHUNKS = 2
LOADS = 2


def dot_nt(a, b):
    return lax.dot_general(a, b, (((1,), (1,)), ((), ())), preferred_element_type=F32)


def hi_lo(x):
    high = x.astype(BF16).astype(F32)
    return jnp.concatenate([high, x - high], axis=0).astype(BF16)


def kernel(
    sizes,
    a_hbm, mask_hbm, w_hbm, e_hbm, ax_hbm, ay_hbm, az_hbm,
    sq_ref, den_ref,
    a_ref, mask_ref, w_ref, e_ref, ax_ref, ay_ref, az_ref, load_sem,
    m_buf, right, own_part, part_out, part_in, w_all, v_out, v_all, q_out, q_all, pack, pack_in, shape_xy, shape_low, shape_z,
    piece_send, piece_recv, fwd_send, part_send, part_recv,
    w_send, w_recv, v_send, v_recv, q_send, q_recv, pack_send, pack_recv,
):
    nr, nc, nl = sizes
    ratio = nr // nc
    rows, cols = a_ref.shape
    width = cols // nl
    atoms = rows // BLOCK
    r, c, l = lax.axis_index("row"), lax.axis_index("col"), lax.axis_index("layer")
    sibling = r + 1 - 2 * (r % 2)
    following = (r + 1) % nr

    def remote(src, dst, send, recv, device):
        return pltpu.make_async_remote_copy(
            src_ref=src, dst_ref=dst, send_sem=send, recv_sem=recv,
            device_id=device, device_id_type=MESH,
        )

    chunks = width // LANES
    tall = rows // LOADS
    small = [
        pltpu.make_async_copy(src, dst, load_sem.at[at])
        for at, (src, dst) in enumerate((
            (mask_hbm, mask_ref), (w_hbm, w_ref), (e_hbm, e_ref),
            (ax_hbm, ax_ref), (ay_hbm, ay_ref), (az_hbm, az_ref),
        ))
    ]
    large = [
        pltpu.make_async_copy(
            a_hbm.at[pl.ds(p * tall, tall), :], a_ref.at[pl.ds(p * tall, tall), :], load_sem.at[6 + p]
        )
        for p in range(LOADS)
    ]
    for copy in small + large:
        copy.start()

    barrier = pltpu.get_barrier_semaphore()
    peers = 0
    for dr in range(nr):
        for dc in range(nc):
            if dr or dc:
                peers += 1
                pl.semaphore_signal(
                    barrier, inc=1, device_id=((r + dr) % nr, (c + dc) % nc, l), device_id_type=MESH
                )
    for k in range(1, nl):
        peers += 1
        pl.semaphore_signal(barrier, inc=1, device_id=(r, c, (l + k) % nl), device_id_type=MESH)

    for copy in small:
        copy.wait()
    kept = jnp.where(mask_ref[...] > 0, 1.0, 0.0).astype(F32)
    spread = lax.broadcasted_iota(jnp.int32, (cols // BLOCK, cols), 1) // BLOCK
    pick = lax.broadcasted_iota(jnp.int32, (cols // BLOCK, cols), 0)
    wide = jnp.dot(kept, jnp.where(spread == pick, 1.0, 0.0).astype(F32), preferred_element_type=F32)
    w_all[l] = jnp.broadcast_to(w_ref[...], (8, width))
    lane_atom = lax.broadcasted_iota(jnp.int32, (8, rows), 1) // BLOCK
    sub = lax.broadcasted_iota(jnp.int32, (8, rows), 0)
    table = jnp.broadcast_to(e_ref[...], (8, rows))
    for j in range(atoms):
        here = lane_atom == j
        for at, ref in ((1, ax_ref), (2, ay_ref), (3, az_ref)):
            table = jnp.where(here & (sub == at), ref[j].astype(F32), table)
    pack[...] = table
    for b in range(atoms):
        if b % (atoms // LOADS) == 0:
            large[b // (atoms // LOADS)].wait()
        at = pl.ds(b * BLOCK, BLOCK)
        m_buf[at, :] = a_ref[at, :] * jnp.broadcast_to(wide[b : b + 1, :], (BLOCK, cols)).astype(BF16)

    pl.semaphore_wait(barrier, peers)

    w_copies = [
        remote(w_all.at[l], w_all.at[l], w_send.at[k - 1], w_recv.at[k - 1], (r, c, (l + k) % nl))
        for k in range(1, nl)
    ]
    for copy in w_copies:
        copy.start()
    pack_copy = remote(pack, pack_in, pack_send.at[0], pack_recv.at[0], (following, c, l))
    pack_copy.start()

    home = r // ratio
    slot = r % ratio

    def strip(h):
        return m_buf.at[:, pl.ds(pl.multiple_of(l * width + h * LANES, LANES), LANES)]

    def piece(i, cc, h):
        return right.at[i, cc, h]

    def sem_at(i, cc, h):
        return (i * nc + cc) * chunks + h

    def piece_copy(k, h):
        return remote(
            strip(h), piece(slot, c, h), piece_send.at[k * chunks + h],
            piece_recv.at[sem_at(slot, c, h)], ((r + 2 * k) % nr, home, l),
        )

    def own_copy(h):
        return pltpu.make_async_copy(strip(h), piece(slot, c, h), piece_recv.at[sem_at(slot, c, h)])

    at_home = home == c
    def start_strips(h):
        for k in range(1, nr // 2):
            piece_copy(k, h).start()

        @pl.when(at_home)
        def _():
            own_copy(h).start()

        @pl.when(jnp.logical_not(at_home))
        def _():
            piece_copy(0, h).start()

    start_strips(0)

    y_first = (c * nl + l) * SY
    y_count = nc * nl * SY

    def profiles(g, ref):
        rate = ref[0:1, :] * (-STEP_SQ)

        def profile(t):
            value = jnp.exp(rate * (t - 7.5) * (t - 7.5))
            return jnp.where((t >= 0.0) & (t < float(TILE)), value, 0.0)

        tx = lax.broadcasted_iota(jnp.int32, (SX, rows), 0).astype(F32) + float(g * SX) - ref[1:2, :]
        ty = (lax.broadcasted_iota(jnp.int32, (SY, rows), 0) + y_first).astype(F32) - ref[2:3, :]
        ty = jnp.where(ty < 0.0, ty + float(y_count), ty)
        tz = lax.broadcasted_iota(jnp.int32, (GZ, rows), 0).astype(F32) - ref[3:4, :]
        tz = jnp.where(tz < 0.0, tz + float(GZ), tz)
        px, py = profile(tx), profile(ty)
        for x in range(SX):
            plane = px[x : x + 1, :] * py
            high = plane.astype(BF16)
            shape_xy[g, x * SY : (x + 1) * SY, :] = high
            shape_low[g, x * SY : (x + 1) * SY, :] = (plane - high.astype(F32)).astype(BF16)
        shape_z[g] = profile(tz)

    profiles(0, pack)

    for copy in w_copies:
        copy.wait_recv()
    total = jnp.zeros((16, rows), F32)
    for k in range(nl):
        total = total + dot_nt(hi_lo(w_all[k]), m_buf[:, k * width : (k + 1) * width])
    v_out[...] = total[:8] + total[8:]

    def v_copy(k):
        return remote(
            v_out, v_all.at[slot, c], v_send.at[k], v_recv.at[slot * nc + c], ((r + k) % nr, home, l)
        )

    @pl.when(at_home)
    def _():
        v_all[slot, c] = v_out[...]

    @pl.when(jnp.logical_not(at_home))
    def _():
        v_copy(0).start()

    for k in range(1, nr):
        v_copy(k).start()
    for h in range(1, chunks):
        start_strips(h)

    pack_copy.wait_recv()
    profiles(1, pack_in)

    def direct(i):
        return (c * ratio + i) % 2 == r % 2

    def fwd_copy(i, cc, h):
        return remote(
            piece(i, cc, h), piece(i, cc, h), fwd_send.at[sem_at(i, cc, h)],
            piece_recv.at[sem_at(i, cc, h)], (sibling, c, l),
        )

    def landed(i, cc, h):
        fwd_copy(i, cc, h).wait_recv()

    def pass_on(h):
        for k in range(nc):
            cc = (c + 1 + k) % nc
            for i in range(ratio):

                @pl.when(direct(i))
                def _():
                    mine = (c * ratio + i == r) & (cc == c)

                    @pl.when(mine)
                    def _():
                        own_copy(h).wait()

                    @pl.when(jnp.logical_not(mine))
                    def _():
                        landed(i, cc, h)

                    fwd_copy(i, cc, h).start()

    def take(cc, h):
        for i in range(ratio):

            @pl.when(jnp.logical_not(direct(i)))
            def _():
                landed(i, cc, h)

    low = rows // OUT_CHUNKS

    def product(cc, h, at):
        total = jnp.dot(m_buf[at, 0:rows], right[0, cc, h], preferred_element_type=F32)
        for i in range(1, ratio):
            total = total + jnp.dot(
                m_buf[at, i * rows : (i + 1) * rows], right[i, cc, h], preferred_element_type=F32
            )
        return total

    def part_copy(k, h, o):
        at = pl.ds(o * low, low)
        index = ((k - 1) * chunks + h) * OUT_CHUNKS + o
        return remote(
            part_out.at[k - 1, h, at, :], part_in.at[k - 1, h, at, :], part_send.at[index],
            part_recv.at[index], (r, (c + k) % nc, l),
        )

    def parts(h):
        for k in range(1, nc):
            take((c + k) % nc, h)
            for o in range(OUT_CHUNKS):
                at = pl.ds(o * low, low)
                part_out[k - 1, h, at, :] = product((c + k) % nc, h, at).astype(BF16)
                part_copy(k, h, o).start()

    def charge_share():
        for i in range(ratio):
            for cc in range(nc):

                @pl.when(jnp.logical_not((c * ratio + i == r) & (cc == c)))
                def _():
                    remote(
                        v_out, v_all.at[i, cc], v_send.at[0], v_recv.at[i * nc + cc], (r, c, l)
                    ).wait_recv()

        total = jnp.zeros((16, rows), F32)
        for i in range(ratio):
            v = v_all[i, 0]
            for cc in range(1, nc):
                v = v + v_all[i, cc]
            total = total + dot_nt(hi_lo(v), m_buf[:, i * rows : (i + 1) * rows])
        q_out[...] = total[:8] + total[8:]
        q_all[0, c] = q_out[...]

    def q_copy(g, k):
        return remote(
            q_out, q_all.at[g, c], q_send.at[g * nc + k], q_recv.at[g * nc + k],
            ((r + g) % nr, (c + k) % nc, l),
        )

    sent_q = [(g, k) for g in range(2) for k in range(nc) if g or k]
    for h in range(chunks):
        pass_on(h)
        if h == 0:
            charge_share()
            for g, k in sent_q:
                q_copy(g, k).start()
        parts(h)

    for h in range(chunks):
        take(c, h)
        for o in range(OUT_CHUNKS):
            at = pl.ds(o * low, low)
            own_part[h, at, :] = product(c, h, at)

    for g, k in sent_q:
        q_copy(g, k).wait_recv()
    total = jnp.zeros((SX * SY, GZ), F32)
    for g in range(2):
        charge = q_all[g, 0]
        for cc in range(1, nc):
            charge = charge + q_all[g, cc]
        value = shape_z[g] * charge[0:1, :]
        high = value.astype(BF16)
        rest = (value - high.astype(F32)).astype(BF16)
        total = total + dot_nt(shape_xy[g], high) + dot_nt(shape_xy[g], rest) + dot_nt(shape_low[g], high)
    den_ref[...] = total.reshape(SX, SY, GZ)

    for h in range(chunks):
        for o in range(OUT_CHUNKS):
            at = pl.ds(o * low, low)
            total = own_part[h, at, :]
            for k in range(1, nc):
                part_copy(k, h, o).wait_recv()
                total = total + part_in[k - 1, h, at, :].astype(F32)
            sq_ref[at, h * LANES : (h + 1) * LANES] = total.astype(BF16)

    for copy in w_copies:
        copy.wait_send()
    pack_copy.wait_send()
    for k in range(1, nr):
        v_copy(k).wait_send()
    for g, k in sent_q:
        q_copy(g, k).wait_send()
    for h in range(chunks):
        for k in range(1, nr // 2):
            piece_copy(k, h).wait_send()
        for i in range(ratio):
            for cc in range(nc):

                @pl.when(direct(i))
                def _():
                    fwd_copy(i, cc, h).wait_send()

    @pl.when(jnp.logical_not(at_home))
    def _():
        v_copy(0).wait_send()
        for h in range(chunks):
            piece_copy(0, h).wait_send()

    for k in range(1, nc):
        for h in range(chunks):
            for o in range(OUT_CHUNKS):
                part_copy(k, h, o).wait_send()


def store(sq_ref, den_ref, sq_out, den_out, sem):
    copies = [
        pltpu.make_async_copy(sq_ref, sq_out, sem.at[0]),
        pltpu.make_async_copy(den_ref, den_out, sem.at[1]),
    ]
    for copy in copies:
        copy.start()
    for copy in copies:
        copy.wait()


def local(sizes, density_matrix, block_mask, weights, exponents, anchor_x, anchor_y, anchor_z):
    nr, nc, nl = sizes
    ratio = nr // nc
    rows, cols = density_matrix.shape
    width = cols // nl
    dma = pltpu.SemaphoreType.DMA
    chunks = width // LANES
    pieces = ratio * nc * chunks
    outs = (nc - 1) * chunks * OUT_CHUNKS
    hbm = pl.BlockSpec(memory_space=pltpu.HBM)
    vmem = pl.BlockSpec(memory_space=pltpu.VMEM)
    inputs = (
        density_matrix, block_mask, weights.reshape(1, -1), exponents.reshape(1, -1),
        anchor_x, anchor_y, anchor_z,
    )
    shapes = (
        jax.ShapeDtypeStruct((rows, width), BF16),
        jax.ShapeDtypeStruct((SX, SY, GZ), F32),
    )
    results = pl.pallas_call(
        functools.partial(kernel, sizes),
        out_shape=(pltpu.VMEM((rows, width), BF16), pltpu.VMEM((SX, SY, GZ), F32)),
        in_specs=[hbm] * 7,
        out_specs=(vmem, vmem),
        scratch_shapes=[
            pltpu.VMEM((rows, cols), BF16),
            pltpu.VMEM(block_mask.shape, jnp.int32),
            pltpu.VMEM((1, width), F32),
            pltpu.VMEM((1, rows), F32),
            pltpu.SMEM(anchor_x.shape, jnp.int32),
            pltpu.SMEM(anchor_x.shape, jnp.int32),
            pltpu.SMEM(anchor_x.shape, jnp.int32),
            dma((6 + LOADS,)),
            pltpu.VMEM((rows, cols), BF16),
            pltpu.VMEM((ratio, nc, chunks, rows, LANES), BF16),
            pltpu.VMEM((chunks, rows, LANES), F32),
            pltpu.VMEM((nc - 1, chunks, rows, LANES), BF16),
            pltpu.VMEM((nc - 1, chunks, rows, LANES), BF16),
            pltpu.VMEM((nl, 8, width), F32),
            pltpu.VMEM((8, rows), F32),
            pltpu.VMEM((ratio, nc, 8, rows), F32),
            pltpu.VMEM((8, rows), F32),
            pltpu.VMEM((2, nc, 8, rows), F32),
            pltpu.VMEM((8, rows), F32),
            pltpu.VMEM((8, rows), F32),
            pltpu.VMEM((2, SX * SY, rows), BF16),
            pltpu.VMEM((2, SX * SY, rows), BF16),
            pltpu.VMEM((2, GZ, rows), F32),
            dma((nr // 2 * chunks,)),
            dma((pieces,)),
            dma((pieces,)),
            dma((outs,)),
            dma((outs,)),
            dma((nl - 1,)),
            dma((nl - 1,)),
            dma((nr,)),
            dma((ratio * nc,)),
            dma((2 * nc,)),
            dma((2 * nc,)),
            dma((1,)),
            dma((1,)),
        ],
        compiler_params=pltpu.CompilerParams(
            collective_id=0, has_side_effects=True, vmem_limit_bytes=66_000_000
        ),
        name="square_collocate",
    )(*[pltpu.with_memory_space_constraint(x, pltpu.HBM) for x in inputs])
    return pl.pallas_call(
        store,
        out_shape=shapes,
        in_specs=[vmem] * 2,
        out_specs=(hbm, hbm),
        scratch_shapes=[dma((2,))],
        compiler_params=pltpu.CompilerParams(vmem_limit_bytes=4 * 1024 * 1024),
        name="store",
    )(*results)


def solution(mesh):
    sizes = (mesh.shape["row"], mesh.shape["col"], mesh.shape["layer"])
    return jax.shard_map(
        functools.partial(local, sizes),
        mesh=mesh,
        in_specs=(
            P("row", "col"), P("row", "col"), P(("col", "layer")),
            P("row"), P("row"), P("row"), P("row"),
        ),
        out_specs=(P("row", ("col", "layer")), P("row", ("col", "layer"), None)),
        check_vma=False,
    )
```
